128 devices in a mesh: layer: 128 (over x, y, z, core).
Axes of the slice: x: 4, y: 4, z: 4, core: 2. Of those that a mesh axis runs over, the one named last changes fastest.
Arguments:
- lower_block: float32 [128, 512, 512], P('layer'), may hold values from -0.109375 to 0.109375
- upper_block: float32 [128, 512, 512], P('layer'), may hold values from -0.109375 to 0.109375
- right_side: float32 [128, 64, 512], P('layer'), may hold values from -6 to 6
Outputs:
- reduced_lower: float32 [128, 512, 512], P('layer')
- reduced_upper: float32 [128, 512, 512], P('layer')
- reduced_rhs: float32 [128, 64, 512], P('layer')
The draws below stay inside these ranges and needn't reach their ends.
All inputs are finite; a program needn't handle non-finite values.
Results may differ from the reference program's by a relative error of at most 0.00022.
Values sent between devices are 32-bit elements; how exact they have to be, the bound alone decides.
No kernel may reach another device: no remote copies, remote signals or barrier semaphores. Data moves between devices by JAX's collectives and lax.ppermute only.
A program may use at most 64 MiB of HBM per device.

```python
import math
import jax
import jax.numpy as jnp
from jax import lax

BLOCK = 512
COLUMNS = 64
LEVELS = 3
CHAINS = 8
LAYERS = 128


def block_scale(key, dims, shards, low, largest):
    level, own = 1.0, jax.random.fold_in(key, 6)
    for axis_at, blocks in shards:
        draws = jnp.exp(jax.random.uniform(jax.random.fold_in(own, axis_at), (blocks,), jnp.float32, low / len(shards), largest / len(shards)))
        level = level * jnp.repeat(draws, dims[axis_at] // blocks).reshape([-1 if axis == axis_at else 1 for axis in range(len(dims))])
    return level


def normal_values(key, dims, deviation, bound, pieces=(), kind=jnp.bfloat16):
    factor_of = block_scale(key, dims, pieces, -0.22, 0.18) if pieces else 1.0
    drawn = jax.random.normal(key, dims, jnp.float32) * deviation * factor_of
    return jnp.minimum(jnp.maximum(drawn, -bound), bound).astype(kind)


def setup_inputs(seed: int = 0) -> dict:
    key_list = jax.random.split(jax.random.key(seed), 4)
    lower_block = normal_values(key_list[0], (LAYERS, BLOCK, BLOCK), (6 * BLOCK) ** -0.5, 0.109375, ((0, 128),), jnp.float32)
    upper_block = normal_values(key_list[1], (LAYERS, BLOCK, BLOCK), (6 * BLOCK) ** -0.5, 0.109375, ((0, 128),), jnp.float32)
    right_side = normal_values(key_list[2], (LAYERS, COLUMNS, BLOCK), 1.0, 6.0, ((0, 128),), jnp.float32)
    return dict(lower_block=lower_block, upper_block=upper_block, right_side=right_side)


def matmul_high(left, right):
    return jnp.dot(left, right, precision=lax.Precision.HIGHEST, preferred_element_type=jnp.float32)

def rows_times(block, columns):
    return lax.dot_general(columns, block, (((1,), (1,)), ((), ())), precision=lax.Precision.HIGHEST, preferred_element_type=jnp.float32)

def reduce_level(group):
    own, from_below, from_above = group
    own_lower = own[:BLOCK]
    own_upper = own[BLOCK:2 * BLOCK]
    own_rhs = own[2 * BLOCK:]
    identity = jnp.eye(BLOCK, dtype=jnp.float32)
    diagonal = identity - matmul_high(own_lower, from_below[BLOCK:2 * BLOCK]) - matmul_high(own_upper, from_above[:BLOCK])
    initial = 2.0 * identity - diagonal
    inverse = matmul_high(initial, 2.0 * identity - matmul_high(diagonal, initial))
    new_lower = -matmul_high(inverse, matmul_high(own_lower, from_below[:BLOCK]))
    new_upper = -matmul_high(inverse, matmul_high(own_upper, from_above[BLOCK:2 * BLOCK]))
    new_rhs = own_rhs - rows_times(own_lower, from_below[2 * BLOCK:]) - rows_times(own_upper, from_above[2 * BLOCK:])
    new_rhs = rows_times(inverse, new_rhs)
    return jnp.concatenate([new_lower, new_upper, new_rhs], axis=0)

def reference(lower_block, upper_block, right_side):
    layers = lower_block.shape[0]
    payload = jnp.concatenate([lower_block, upper_block, right_side], axis=1)
    for level_index in range(LEVELS):
        stride = 2 ** level_index
        from_below = jnp.roll(payload, stride, axis=0)
        from_above = jnp.roll(payload, -stride, axis=0)
        payload = lax.map(reduce_level, (payload, from_below, from_above))
    chain_len = layers // CHAINS
    payload = payload.reshape(chain_len, CHAINS, payload.shape[1], payload.shape[2])
    payload = jnp.transpose(payload, (1, 0, 2, 3)).reshape(layers, payload.shape[2], payload.shape[3])
    factor = 2.5 ** 8 * math.sqrt(BLOCK)
    return (payload[:, :BLOCK] * factor, payload[:, BLOCK:2 * BLOCK] * factor, payload[:, 2 * BLOCK:])
```

```python
import math

import jax
import jax.numpy as jnp
from jax import lax
from jax.sharding import PartitionSpec as P

BLOCK = 512
CHAINS = 8
LAYERS = 128
HIGH = lax.Precision.HIGH

LAST_LEVEL_BITS = ((6,), (0, 1, 5), (4,), (3,), (0, 1, 3, 4), (0, 3, 4, 5, 6), (1, 2, 3, 4, 5))


def last_level_device(layer):
    device = 0
    for bits in LAST_LEVEL_BITS:
        device = 2 * device + sum(layer >> bit for bit in bits) % 2
    return device ^ 2


def start_device(layer):
    return layer


def final_device(layer):
    return layer % CHAINS * (LAYERS // CHAINS) + layer // CHAINS


def move(value, source, target, partner=lambda layer: layer):
    pairs = [(source(i), target(partner(i) % LAYERS)) for i in range(LAYERS)]
    return lax.ppermute(value, "layer", pairs)


def stack(block, rhs):
    return jnp.concatenate([block, rhs], axis=0)


def matmul(left, right):
    return jnp.dot(left, right, precision=HIGH, preferred_element_type=jnp.float32)


def rows_times(block, columns):
    return lax.dot_general(
        columns,
        block,
        (((1,), (1,)), ((), ())),
        precision=HIGH,
        preferred_element_type=jnp.float32,
    )


def reduce_level(first, second, rhs, couple_first, couple_second, next_first, next_second):
    identity = jnp.eye(BLOCK, dtype=jnp.float32)
    coupling = matmul(first, couple_first) + matmul(second, couple_second)
    square = matmul(coupling, coupling)
    inverse = identity + coupling + square + matmul(coupling, square)
    inverse_first = matmul(inverse, first)
    inverse_second = matmul(inverse, second)
    new_second = -matmul(inverse_second, next_second[:BLOCK])
    new_first = -matmul(inverse_first, next_first[:BLOCK])
    new_rhs = (
        rows_times(inverse, rhs)
        - rows_times(inverse_first, next_first[BLOCK:])
        - rows_times(inverse_second, next_second[BLOCK:])
    )
    return new_first, new_second, new_rhs


def pair_level(first, second, rhs, place, bit):
    stride = 1 << bit

    def near(value):
        return move(value, place, place, lambda i: i ^ stride)

    def far(value):
        return move(value, place, place, lambda i: i + stride if i & stride else i - stride)

    couple_first = far(first)
    couple_second = near(second)
    next_first = far(stack(second, rhs))
    next_second = near(stack(first, rhs))
    return reduce_level(
        first, second, rhs, couple_first, couple_second, next_first, next_second
    )


def line_level(first, second, rhs, place, stride):
    def one(value):
        return move(value, place, place, lambda i: i - stride if i % 2 else i + stride)

    def two(value):
        return move(value, place, place, lambda i: i + stride if i % 2 else i - stride)

    couple_first = one(second)
    couple_second = two(first)
    next_first = one(stack(first, rhs))
    next_second = two(stack(second, rhs))
    return reduce_level(
        first, second, rhs, couple_first, couple_second, next_first, next_second
    )


def choose(condition, one, two):
    return jnp.where(condition, one, two), jnp.where(condition, two, one)


def per_device(lower_block, upper_block, right_side):
    layer = lax.axis_index("layer")
    rhs = right_side[0]
    first, second = choose(layer & 1 == 0, lower_block[0], upper_block[0])
    first, second, rhs = pair_level(first, second, rhs, start_device, 0)
    first, second, rhs = line_level(first, second, rhs, start_device, 2)
    first, second = choose((layer ^ (layer >> 2)) & 1 == 0, first, second)
    first = move(first, start_device, last_level_device)
    second_rhs = move(stack(second, rhs), start_device, last_level_device)
    second, rhs = second_rhs[:BLOCK], second_rhs[BLOCK:]
    first, second, rhs = pair_level(first, second, rhs, last_level_device, 2)
    first = move(first, last_level_device, final_device)
    second_rhs = move(stack(second, rhs), last_level_device, final_device)
    factor = 2.5**8 * math.sqrt(BLOCK)
    lower, upper = choose(layer & LAYERS // 2 == 0, first, second_rhs[:BLOCK])
    return (lower[None] * factor, upper[None] * factor, second_rhs[None, BLOCK:])


def solution(mesh):
    placed = (P("layer", None, None), P("layer", None, None), P("layer", None, None))
    return jax.shard_map(
        per_device,
        mesh=mesh,
        in_specs=placed,
        out_specs=placed,
        check_vma=False,
    )
```

```python
import math

import jax
import jax.numpy as jnp
from jax import lax
from jax.sharding import PartitionSpec as P

BLOCK = 512
CHAINS = 8
LAYERS = 128
HIGH, HIGHEST = lax.Precision.HIGH, lax.Precision.HIGHEST

LAST_LEVEL_BITS = ((6,), (0, 1, 5), (4,), (3,), (0, 1, 3, 4), (0, 3, 4, 5, 6), (1, 2, 3, 4, 5))


def last_level_device(layer):
    device = 0
    for bits in LAST_LEVEL_BITS:
        device = 2 * device + sum(layer >> bit for bit in bits) % 2
    return device ^ 2


def start_device(layer):
    return layer


def final_device(layer):
    return layer % CHAINS * (LAYERS // CHAINS) + layer // CHAINS


def move(value, source, target, partner=lambda layer: layer):
    pairs = [(source(i), target(partner(i) % LAYERS)) for i in range(LAYERS)]
    return lax.ppermute(value, "layer", pairs)


def stack(block, rhs):
    return jnp.concatenate([block, rhs], axis=0)


def matmul(left, right, precision=HIGH):
    return jnp.dot(left, right, precision=precision, preferred_element_type=jnp.float32)


def rows_times(block, columns):
    return lax.dot_general(
        columns,
        block,
        (((1,), (1,)), ((), ())),
        precision=HIGH,
        preferred_element_type=jnp.float32,
    )


def reduce_level(
    first, second, rhs, couple_first, couple_second, next_first, next_second, precision
):
    identity = jnp.eye(BLOCK, dtype=jnp.float32)
    coupling = matmul(first, couple_first) + matmul(second, couple_second)
    square = matmul(coupling, coupling)
    inverse = identity + coupling + square + matmul(coupling, square)
    inverse_first = matmul(inverse, first, precision)
    inverse_second = matmul(inverse, second, precision)
    new_second = -matmul(inverse_second, next_second[:BLOCK])
    new_first = -matmul(inverse_first, next_first[:BLOCK])
    new_rhs = (
        rows_times(inverse, rhs)
        - rows_times(inverse_first, next_first[BLOCK:])
        - rows_times(inverse_second, next_second[BLOCK:])
    )
    return new_first, new_second, new_rhs


def pair_level(first, second, rhs, place, bit, precision):
    stride = 1 << bit

    def near(value):
        return move(value, place, place, lambda i: i ^ stride)

    def far(value):
        return move(value, place, place, lambda i: i + stride if i & stride else i - stride)

    couple_first = far(first)
    couple_second = near(second)
    next_first = far(stack(second, rhs))
    next_second = near(stack(first, rhs))
    return reduce_level(
        first, second, rhs, couple_first, couple_second, next_first, next_second, precision
    )


def line_level(first, second, rhs, place, stride):
    def one(value):
        return move(value, place, place, lambda i: i - stride if i % 2 else i + stride)

    def two(value):
        return move(value, place, place, lambda i: i + stride if i % 2 else i - stride)

    couple_first = one(second)
    couple_second = two(first)
    next_first = one(stack(first, rhs))
    next_second = two(stack(second, rhs))
    return reduce_level(
        first, second, rhs, couple_first, couple_second, next_first, next_second, HIGHEST
    )


def choose(condition, one, two):
    return jnp.where(condition, one, two), jnp.where(condition, two, one)


def per_device(lower_block, upper_block, right_side):
    layer = lax.axis_index("layer")
    rhs = right_side[0]
    first, second = choose(layer & 1 == 0, lower_block[0], upper_block[0])
    first, second, rhs = pair_level(first, second, rhs, start_device, 0, HIGHEST)
    first, second, rhs = line_level(first, second, rhs, start_device, 2)
    first, second = choose((layer ^ (layer >> 2)) & 1 == 0, first, second)
    first = move(first, start_device, last_level_device)
    second_rhs = move(stack(second, rhs), start_device, last_level_device)
    second, rhs = second_rhs[:BLOCK], second_rhs[BLOCK:]
    first, second, rhs = pair_level(first, second, rhs, last_level_device, 2, HIGH)
    first = move(first, last_level_device, final_device)
    second_rhs = move(stack(second, rhs), last_level_device, final_device)
    factor = 2.5**8 * math.sqrt(BLOCK)
    lower, upper = choose(layer & LAYERS // 2 == 0, first, second_rhs[:BLOCK])
    return (lower[None] * factor, upper[None] * factor, second_rhs[None, BLOCK:])


def solution(mesh):
    placed = (P("layer", None, None), P("layer", None, None), P("layer", None, None))
    return jax.shard_map(
        per_device,
        mesh=mesh,
        in_specs=placed,
        out_specs=placed,
        check_vma=False,
    )
```

```python
import math

import jax
import jax.numpy as jnp
from jax import lax
from jax.sharding import PartitionSpec as P

BLOCK = 512
CHAINS = 8
LAYERS = 128
HIGH, HIGHEST = lax.Precision.HIGH, lax.Precision.HIGHEST

LAST_LEVEL_BITS = ((6,), (0, 1, 5), (4,), (3,), (0, 1, 3, 4), (0, 3, 4, 5, 6), (1, 2, 3, 4, 5))


def last_level_device(layer):
    device = 0
    for bits in LAST_LEVEL_BITS:
        device = 2 * device + sum(layer >> bit for bit in bits) % 2
    return device ^ 2


def start_device(layer):
    return layer


def final_device(layer):
    return layer % CHAINS * (LAYERS // CHAINS) + layer // CHAINS


def move(value, source, target, partner=lambda layer: layer):
    pairs = [(source(i), target(partner(i) % LAYERS)) for i in range(LAYERS)]
    return lax.ppermute(value, "layer", pairs)


def stack(block, rhs):
    return jnp.concatenate([block, rhs], axis=0)


def matmul(left, right, precision=HIGH):
    return jnp.dot(left, right, precision=precision, preferred_element_type=jnp.float32)


def rows_times(block, columns):
    return lax.dot_general(
        columns,
        block,
        (((1,), (1,)), ((), ())),
        precision=HIGH,
        preferred_element_type=jnp.float32,
    )


def reduce_level(
    first, second, rhs, couple_first, couple_second, next_first, next_second, precision
):
    identity = jnp.eye(BLOCK, dtype=jnp.float32)
    coupling = matmul(first, couple_first) + matmul(second, couple_second)
    square = matmul(coupling, coupling)
    inverse = identity + coupling + square + matmul(coupling, square)
    inverse_first = matmul(inverse, first, precision)
    inverse_second = matmul(inverse, second, precision)
    new_second = -matmul(inverse_second, next_second[:BLOCK])
    new_first = -matmul(inverse_first, next_first[:BLOCK])
    new_rhs = (
        rows_times(inverse, rhs)
        - rows_times(inverse_first, next_first[BLOCK:])
        - rows_times(inverse_second, next_second[BLOCK:])
    )
    return new_first, new_second, new_rhs


def pair_level(first, second, rhs, place, bit, precision):
    stride = 1 << bit

    def near(value):
        return move(value, place, place, lambda i: i ^ stride)

    def far(value):
        return move(value, place, place, lambda i: i + stride if i & stride else i - stride)

    couple_first = far(first)
    couple_second = near(second)
    next_first = far(stack(second, rhs))
    next_second = near(stack(first, rhs))
    return reduce_level(
        first, second, rhs, couple_first, couple_second, next_first, next_second, precision
    )


def last_level(first_rhs, second):
    place = last_level_device

    def near(value):
        return move(value, place, place, lambda i: i ^ 4)

    def far(value):
        return move(value, place, place, lambda i: i + 4 if i & 4 else i - 4)

    couple_first = far(first_rhs)
    couple_second = near(second)
    next_first = stack(far(second), couple_first[BLOCK:])
    next_second = near(first_rhs)
    return reduce_level(
        first_rhs[:BLOCK],
        second,
        first_rhs[BLOCK:],
        couple_first[:BLOCK],
        couple_second,
        next_first,
        next_second,
        HIGH,
    )


def line_level(first, second, rhs, place, stride):
    def one(value):
        return move(value, place, place, lambda i: i - stride if i % 2 else i + stride)

    def two(value):
        return move(value, place, place, lambda i: i + stride if i % 2 else i - stride)

    couple_first = one(second)
    couple_second = two(first)
    next_first = one(stack(first, rhs))
    next_second = two(stack(second, rhs))
    return reduce_level(
        first, second, rhs, couple_first, couple_second, next_first, next_second, HIGHEST
    )


def choose(condition, one, two):
    return jnp.where(condition, one, two), jnp.where(condition, two, one)


def per_device(lower_block, upper_block, right_side):
    layer = lax.axis_index("layer")
    rhs = right_side[0]
    first, second = choose(layer & 1 == 0, lower_block[0], upper_block[0])
    first, second, rhs = pair_level(first, second, rhs, start_device, 0, HIGHEST)
    first, second, rhs = line_level(first, second, rhs, start_device, 2)
    first, second = choose((layer ^ (layer >> 2)) & 1 == 0, first, second)
    first_rhs = move(stack(first, rhs), start_device, last_level_device)
    second = move(second, start_device, last_level_device)
    first, second, rhs = last_level(first_rhs, second)
    second = move(second, last_level_device, final_device)
    first = move(first, last_level_device, final_device)
    rhs = move(rhs, last_level_device, final_device)
    factor = 2.5**8 * math.sqrt(BLOCK)
    lower, upper = choose(layer & LAYERS // 2 == 0, first, second)
    return (lower[None] * factor, upper[None] * factor, rhs[None])


def solution(mesh):
    placed = (P("layer", None, None), P("layer", None, None), P("layer", None, None))
    return jax.shard_map(
        per_device,
        mesh=mesh,
        in_specs=placed,
        out_specs=placed,
        check_vma=False,
    )
```
